512 devices in a mesh: atoms: 128 (over z, y_hi, x, core), kpt: 4 (over y_lo).
Axes of the slice: x: 4, y: 8 (y_hi: 2, y_lo: 4; y = y_hi * 4 + y_lo), z: 8, core: 2. Of those that a mesh axis runs over, the one named last changes fastest.
Arguments:
- blocks: bfloat16 [4608, 32, 13, 13], P('atoms', 'kpt'), may hold values from -0.3125 to 0.3125
- vectors: bfloat16 [8, 4608, 2, 13, 128], P('kpt', 'atoms'), may hold values from -6 to 6
- kvecs: float32 [8, 2], replicated, may hold values from 0 to 1
- neighbours: int32 [4608, 32], P('atoms'), may hold values from 0 to 4607, as said below
- offsets: int32 [4608, 32], P('atoms'), may hold values from 0 to 48
- counts: int32 [4608], P('atoms'), may hold values from 16 to 32
Outputs:
- first: bfloat16 [8, 4608, 2, 13, 128], P('kpt', 'atoms')
- second: bfloat16 [8, 4608, 2, 13, 128], P('kpt', 'atoms')
The draws below stay inside these ranges and needn't reach their ends.
Inputs may be any that keep to these rules, and one draw needn't show every extreme that they name: neighbours[a, s] = (a + d) mod 4608 with -32 <= d <= 32; both d = 32 and d = -32 occur.
All inputs are finite; a program needn't handle non-finite values.
Results may differ from the reference program's by a relative error of at most 0.0063.
Values may be sent and summed in bfloat16 or wider, within the bound.
No kernel may reach another device: no remote copies, remote signals or barrier semaphores. Data moves between devices by JAX's collectives and lax.ppermute only.
A program may use at most 128 MiB of HBM per device.

```python
import math
import jax
import jax.numpy as jnp
from jax import lax

ATOM_ORBITALS = 13
NV = 128
NEIGHBOUR_SLOTS = 32
LATTICE_OFFSETS = 49
NK = 8
NEIGHBOUR_REACH = 32
CELL_ATOMS = 4608


def draw_neighbours(key, part):
    sampled_reach = jax.random.randint(key, (CELL_ATOMS, NEIGHBOUR_SLOTS), -NEIGHBOUR_REACH, NEIGHBOUR_REACH + 1)
    sampled_reach = sampled_reach.at[0, 1].set(NEIGHBOUR_REACH).at[1, 1].set(-NEIGHBOUR_REACH).at[0, 2].set(-1).at[0, 3].set(0)
    return ((jnp.arange(CELL_ATOMS, dtype=jnp.int32)[:, None] + sampled_reach) % CELL_ATOMS).astype(jnp.int32)


def draw_counts(key, part):
    sampled_neighbours = jax.random.randint(key, (CELL_ATOMS,), NEIGHBOUR_SLOTS // 2, NEIGHBOUR_SLOTS + 1)
    return sampled_neighbours.at[0].set(NEIGHBOUR_SLOTS).at[1].set(NEIGHBOUR_SLOTS // 2).astype(jnp.int32)


def touch_ends(array, key, least, top_value):
    spot = [jax.random.randint(jax.random.fold_in(key, axis), (), 0, length) for axis, length in enumerate(array.shape)]
    main_axis = array.shape.index(max(array.shape))
    neighbour = spot[:main_axis] + [(spot[main_axis] + 1) % array.shape[main_axis]] + spot[main_axis + 1:]
    return array.at[tuple(spot)].set(least).at[tuple(neighbour)].set(top_value)


def block_scale(stream_key, extent, split, smallest, high):
    def one(dim, shards_of):
        heights = jax.random.uniform(jax.random.fold_in(jax.random.fold_in(stream_key, 6), dim), (shards_of,), jnp.float32, smallest / len(split), high / len(split))
        return jnp.repeat(jnp.exp(heights), extent[dim] // shards_of).reshape((-1,) + (1,) * (len(extent) - dim - 1))

    level = one(*split[0])
    for cut in split[1:]:
        level = level * one(*cut)
    return level


def bell_draw(rng, dims, width, limit, pieces=(), held_as=jnp.bfloat16):
    loudness = block_scale(rng, dims, pieces, -0.22, 0.18) if pieces else 1.0
    entries = jax.random.normal(rng, dims, jnp.float32) * width * loudness
    return jnp.minimum(jnp.maximum(entries, -limit), limit).astype(held_as)


def setup_inputs(seed: int = 0) -> dict:
    key_list = jax.random.split(jax.random.key(seed), 7)
    return {
        "blocks": bell_draw(key_list[0], (CELL_ATOMS, NEIGHBOUR_SLOTS, ATOM_ORBITALS, ATOM_ORBITALS), (ATOM_ORBITALS * NEIGHBOUR_SLOTS) ** -0.5, 0.3125, ((0, 128), (1, 4))),
        "vectors": bell_draw(key_list[1], (NK, CELL_ATOMS, 2, ATOM_ORBITALS, NV), 1.0, 6.0, ((0, 4), (1, 128))),
        "kvecs": jnp.clip(jax.random.uniform(key_list[2], (NK, 2), jnp.float32, 0.0, 1.0), 0.0, 1.0),
        "neighbours": draw_neighbours(jax.random.fold_in(key_list[6], 71), 0),
        "offsets": touch_ends(jax.random.randint(key_list[4], (CELL_ATOMS, NEIGHBOUR_SLOTS), 0, LATTICE_OFFSETS), jax.random.fold_in(key_list[4], 1), 0, LATTICE_OFFSETS - 1).astype(jnp.int32),
        "counts": draw_counts(jax.random.fold_in(key_list[6], 71), 0),
    }


def angles(kvecs, offsets):
    grid_row = (offsets // 7 - 3).astype(jnp.float32)
    grid_col = (offsets % 7 - 3).astype(jnp.float32)
    return 2.0 * math.pi * (kvecs[:, 0, None, None] * grid_row[None] + kvecs[:, 1, None, None] * grid_col[None])


def phased(kvecs, offsets, counts, blocks):
    theta = angles(kvecs, offsets)
    live_slot = jnp.arange(offsets.shape[1], dtype=jnp.int32)[None, :] < counts[:, None]
    block_f = blocks.astype(jnp.float32)[None]
    cos_part = jnp.where(live_slot[None], jnp.cos(theta), 0.0)[..., None, None]
    sin_part = jnp.where(live_slot[None], jnp.sin(theta), 0.0)[..., None, None]
    return (cos_part * block_f).astype(jnp.bfloat16), (sin_part * block_f).astype(jnp.bfloat16)


def apply_one(real_h, imag_h, vector_k, neighbours):
    def take_slot(running, slot_index):
        picked = vector_k[neighbours[:, slot_index]].astype(jnp.float32)
        real_s = real_h[:, slot_index].astype(jnp.float32)
        imag_s = imag_h[:, slot_index].astype(jnp.float32)
        real_out = jnp.einsum('aop,apv->aov', real_s, picked[:, 0]) - jnp.einsum('aop,apv->aov', imag_s, picked[:, 1])
        imag_out = jnp.einsum('aop,apv->aov', real_s, picked[:, 1]) + jnp.einsum('aop,apv->aov', imag_s, picked[:, 0])
        return running + jnp.stack([real_out, imag_out], axis=1), None
    start_sum = jnp.zeros(vector_k.shape, jnp.float32)
    summed, unused = lax.scan(take_slot, start_sum, jnp.arange(neighbours.shape[1], dtype=jnp.int32))
    return summed.astype(jnp.bfloat16)


def reference(blocks, vectors, kvecs, neighbours, offsets, counts):
    def per_point(packed):
        kvec_one, vector_k = packed
        real_h, imag_h = phased(kvec_one[None], offsets, counts, blocks)
        first_k = apply_one(real_h[0], imag_h[0], vector_k, neighbours)
        second_k = apply_one(real_h[0], imag_h[0], first_k, neighbours)
        return first_k, second_k
    first, second = lax.map(per_point, (kvecs, vectors))
    return (first, second)
```

```python
import math

import jax
import jax.numpy as jnp
from jax import lax
from jax.experimental import pallas as pl
from jax.experimental.pallas import tpu as pltpu
from jax.sharding import PartitionSpec as P

REACH = 32
NO = 13
NV = 128
SLOTS = 32
OWN = 8
LANES = 128
ROWS = 16
VMEM = pl.BlockSpec(memory_space=pltpu.VMEM)
SMEM = pl.BlockSpec(memory_space=pltpu.SMEM)


def pack_kernel(blocks_ref, out_ref, buf):
    atoms = blocks_ref.shape[3]
    buf[...] = jnp.zeros_like(buf)
    r = lax.broadcasted_iota(jnp.int32, (NO * OWN, LANES), 0)
    c = lax.broadcasted_iota(jnp.int32, (NO * OWN, LANES), 1)
    place = ((r % OWN == c // ROWS) & (r // OWN == c % ROWS)).astype(jnp.float32).astype(jnp.bfloat16)
    for x in range(NO):
        b = blocks_ref[x].astype(jnp.float32).reshape(NO * OWN, atoms).astype(jnp.bfloat16)
        t = lax.dot_general(b, place, (((0,), (0,)), ((), ())), preferred_element_type=jnp.float32)
        buf[pl.ds(x, atoms, stride=ROWS), :] = t
    out_ref[...] = buf[...].astype(jnp.bfloat16)


def pack_blocks(blocks):
    atoms = blocks.shape[0]
    return pl.pallas_call(
        pack_kernel,
        out_shape=jax.ShapeDtypeStruct((atoms * ROWS, LANES), jnp.bfloat16),
        in_specs=[VMEM],
        out_specs=VMEM,
        scratch_shapes=[pltpu.VMEM((atoms * ROWS, LANES), jnp.float32)],
        name="pack_blocks",
    )(jnp.transpose(blocks, (2, 3, 1, 0)))


def phase_kernel(kv_ref, spot_ref, offs_ref, counts_ref, b0, b1, b2, b3, h_ref, ce, se):
    atoms = offs_ref.shape[1]
    nk = h_ref.shape[0] // (atoms * 2 * ROWS)
    mine = spot_ref[0]
    offs = offs_ref[...]
    g0 = (offs // 7 - 3).astype(jnp.float32)
    g1 = (offs % 7 - 3).astype(jnp.float32)
    slot = lax.broadcasted_iota(jnp.int32, offs.shape, 0)
    live = slot < counts_ref[...]
    width = 4 * LANES
    r = lax.broadcasted_iota(jnp.int32, (SLOTS, width), 0)
    c = lax.broadcasted_iota(jnp.int32, (SLOTS, width), 1)
    group = (c // LANES + mine) % 4
    spread = (r == group * OWN + (c % LANES) // ROWS).astype(jnp.float32)
    for k in range(nk):
        theta = (2.0 * math.pi) * (kv_ref[nk * mine + k, 0] * g0 + kv_ref[nk * mine + k, 1] * g1)
        for dst, val in ((ce, jnp.cos(theta)), (se, jnp.sin(theta))):
            wide = lax.dot_general(
                jnp.where(live, val, 0.0), spread, (((0,), (0,)), ((), ())),
                precision=lax.Precision.HIGHEST, preferred_element_type=jnp.float32)
            for g in range(4):
                top = (g * nk + k) * atoms
                dst[top:top + atoms, :] = wide[:, g * LANES:(g + 1) * LANES]
    pieces = (b0, b1, b2, b3)

    def one(a, carry):
        for g in range(4):
            lanes = slice(g * LANES, (g + 1) * LANES)
            block = pieces[g][pl.ds(pl.multiple_of(a * ROWS, ROWS), ROWS), :].astype(jnp.float32)
            for k in range(nk):
                row = pl.multiple_of((k * atoms + a) * 2 * ROWS, 2 * ROWS)
                h_ref[pl.ds(row, ROWS), lanes] = (ce[pl.ds((g * nk + k) * atoms + a, 1), :] * block).astype(jnp.bfloat16)
                h_ref[pl.ds(row + ROWS, ROWS), lanes] = (se[pl.ds((g * nk + k) * atoms + a, 1), :] * block).astype(jnp.bfloat16)
        return carry

    lax.fori_loop(0, atoms, one, 0)


def phase_blocks(kvecs, spot, offsets, counts, pieces, nk):
    atoms = offsets.shape[0]
    return pl.pallas_call(
        phase_kernel,
        out_shape=jax.ShapeDtypeStruct((nk * atoms * 2 * ROWS, 4 * LANES), jnp.bfloat16),
        in_specs=[SMEM, SMEM] + [VMEM] * 6,
        out_specs=VMEM,
        scratch_shapes=[pltpu.VMEM((4 * nk * atoms, LANES), jnp.float32)] * 2,
        name="phase_blocks",
    )(kvecs, spot, offsets.T, counts.reshape(1, atoms), *pieces)


def apply_kernel(nbr_ref, spot_ref, h_ref, own_ref, left_ref, right_ref, *rest, halos):
    if halos:
        out_ref, tail_ref, head_ref, flat, win, acc = rest
    else:
        out_ref, flat, win, acc = rest
    atoms = nbr_ref.shape[1]
    nk = h_ref.shape[0] // (atoms * 2 * ROWS)
    window = atoms + 2 * REACH
    edge = REACH * 2 * NO
    mid = atoms * 2 * NO
    span = edge * 2 + mid
    mine = spot_ref[0]
    for k in range(nk):
        flat[k * span:k * span + edge, :] = left_ref[k * edge:(k + 1) * edge, :].astype(jnp.float32)
        flat[k * span + edge:k * span + edge + mid, :] = own_ref[k * mid:(k + 1) * mid, :].astype(jnp.float32)
        flat[k * span + edge + mid:(k + 1) * span, :] = right_ref[k * edge:(k + 1) * edge, :].astype(jnp.float32)
    flat[nk * span:, :] = jnp.zeros((flat.shape[0] - nk * span, NV), jnp.float32)

    def split(i, carry):
        for j in range(4):
            w = i * 4 + j
            for part in range(2):
                win[w, part] = flat[pl.ds(w * 2 * NO + part, ROWS, stride=2), :].astype(jnp.bfloat16)
        return carry

    lax.fori_loop(0, nk * window // 4, split, 0)

    def one(a, carry):
        for k in range(nk):
            row = pl.multiple_of((k * atoms + a) * 2 * ROWS, 2 * ROWS)
            total = None
            for half in range(2):
                tiles = []
                for g in (2 * half, 2 * half + 1):
                    base = ((mine + g) % 4) * OWN
                    for s in range(OWN):
                        w = nbr_ref[base + s, a] + k * window
                        tiles.append(jnp.concatenate([win[w, 0], win[w, 1]], axis=1))
                rhs = jnp.concatenate(tiles, axis=0)
                lhs = h_ref[pl.ds(row, 2 * ROWS), 2 * half * LANES:(2 * half + 2) * LANES]
                got = jnp.dot(lhs, rhs, preferred_element_type=jnp.float32)
                total = got if total is None else total + got
            re = total[:ROWS, :NV] - total[ROWS:, NV:]
            im = total[:ROWS, NV:] + total[ROWS:, :NV]
            start = (k * atoms + a) * 2 * NO
            acc[pl.ds(start, NO, stride=2), :] = re[:NO]
            acc[pl.ds(start + 1, NO, stride=2), :] = im[:NO]
        return carry

    lax.fori_loop(0, atoms, one, 0)
    for k in range(nk):
        base = k * mid
        out_ref[base:base + mid, :] = acc[base:base + mid, :].astype(jnp.bfloat16)
        if halos:
            tail_ref[k * edge:(k + 1) * edge, :] = acc[base + mid - edge:base + mid, :].astype(jnp.bfloat16)
            head_ref[k * edge:(k + 1) * edge, :] = acc[base:base + edge, :].astype(jnp.bfloat16)


def apply_blocks(nbr, spot, h, own, left, right, halos):
    atoms = nbr.shape[1]
    nk = h.shape[0] // (atoms * 2 * ROWS)
    edge = nk * REACH * 2 * NO
    window = atoms + 2 * REACH
    shapes = [jax.ShapeDtypeStruct(own.shape, jnp.bfloat16)]
    if halos:
        shapes += [jax.ShapeDtypeStruct((edge, NV), jnp.bfloat16)] * 2
    return pl.pallas_call(
        lambda *refs: apply_kernel(*refs, halos=halos),
        out_shape=shapes,
        in_specs=[SMEM, SMEM] + [VMEM] * 4,
        out_specs=[VMEM] * len(shapes),
        scratch_shapes=[
            pltpu.VMEM((nk * window * 2 * NO + ROWS, NV), jnp.float32),
            pltpu.VMEM((nk * window, 2, ROWS, NV), jnp.bfloat16),
            pltpu.VMEM((own.shape[0], NV), jnp.float32),
        ],
        name="apply_blocks",
    )(nbr, spot, h, own, left, right)


def exchange(tail, head):
    n = lax.axis_size("atoms")
    left = lax.ppermute(tail, "atoms", [(i, (i + 1) % n) for i in range(n)])
    right = lax.ppermute(head, "atoms", [((i + 1) % n, i) for i in range(n)])
    return left, right


def per_device(blocks, vectors, kvecs, neighbours, offsets, counts):
    atoms = blocks.shape[0]
    nk = vectors.shape[0]
    rows = jnp.transpose(vectors, (0, 1, 3, 2, 4)).reshape(nk * atoms * NO * 2, NV)
    per_k = rows.reshape(nk, atoms * NO * 2, NV)
    edge = REACH * NO * 2
    left, right = exchange(per_k[:, -edge:].reshape(nk * edge, NV), per_k[:, :edge].reshape(nk * edge, NV))
    packed = pack_blocks(blocks)
    owners = lax.axis_size("kpt")
    pieces = [packed] + [
        lax.ppermute(packed, "kpt", [(i, (i - d) % owners) for i in range(owners)]) for d in range(1, owners)
    ]
    spot = lax.axis_index("kpt").astype(jnp.int32).reshape(1)
    total_atoms = atoms * lax.axis_size("atoms")
    base = lax.axis_index("atoms") * atoms - REACH
    nbr = (neighbours.T - base + total_atoms) % total_atoms
    h = phase_blocks(kvecs, spot, offsets, counts, pieces, nk)
    first, tail, head = apply_blocks(nbr, spot, h, rows, left, right, True)
    left, right = exchange(tail, head)
    (second,) = apply_blocks(nbr, spot, h, first, left, right, False)

    def whole(flat):
        return jnp.transpose(flat.reshape(nk, atoms, NO, 2, NV), (0, 1, 3, 2, 4))

    return whole(first), whole(second)


def solution(mesh):
    placed = (
        P("atoms", "kpt", None, None),
        P("kpt", "atoms", None, None, None),
        P(),
        P("atoms", None),
        P("atoms", None),
        P("atoms"),
    )
    return jax.shard_map(
        per_device,
        mesh=mesh,
        in_specs=placed,
        out_specs=(P("kpt", "atoms", None, None, None), P("kpt", "atoms", None, None, None)),
        check_vma=False,
    )
```

```python
import math

import jax
import jax.numpy as jnp
from jax import lax
from jax.experimental import pallas as pl
from jax.experimental.pallas import tpu as pltpu
from jax.sharding import PartitionSpec as P

REACH = 32
NO = 13
NV = 128
SLOTS = 32
OWN = 8
LANES = 128
ROWS = 16
SPLIT = 4
UNROLL = 2
VMEM = pl.BlockSpec(memory_space=pltpu.VMEM)
SMEM = pl.BlockSpec(memory_space=pltpu.SMEM)


def pack_kernel(blocks_ref, out_ref, buf):
    atoms = blocks_ref.shape[3]
    r = lax.broadcasted_iota(jnp.int32, (NO * OWN, LANES), 0)
    c = lax.broadcasted_iota(jnp.int32, (NO * OWN, LANES), 1)
    place = ((r % OWN == c // ROWS) & (r // OWN == c % ROWS)).astype(jnp.float32).astype(jnp.bfloat16)
    for x in range(NO):
        b = blocks_ref[x].astype(jnp.float32).reshape(NO * OWN, atoms).astype(jnp.bfloat16)
        t = lax.dot_general(b, place, (((0,), (0,)), ((), ())), preferred_element_type=jnp.float32)
        buf[pl.ds(x, atoms, stride=NO), :] = t
    out_ref[...] = buf[...].astype(jnp.bfloat16)


def pack_blocks(blocks):
    atoms = blocks.shape[0]
    return pl.pallas_call(
        pack_kernel,
        out_shape=jax.ShapeDtypeStruct((atoms * NO, LANES), jnp.bfloat16),
        in_specs=[VMEM],
        out_specs=VMEM,
        scratch_shapes=[pltpu.VMEM((atoms * NO, LANES), jnp.float32)],
        name="pack_blocks",
    )(jnp.transpose(blocks, (2, 3, 1, 0)))


def phase_kernel(kv_ref, spot_ref, offs_ref, counts_ref, b0, b1, b2, b3, h_ref, ce, se, bf):
    atoms = offs_ref.shape[1]
    nk = h_ref.shape[0] // (atoms * 2 * ROWS)
    mine = spot_ref[0]
    offs = offs_ref[...]
    g0 = (offs // 7 - 3).astype(jnp.float32)
    g1 = (offs % 7 - 3).astype(jnp.float32)
    slot = lax.broadcasted_iota(jnp.int32, offs.shape, 0)
    live = slot < counts_ref[...]
    width = 4 * LANES
    r = lax.broadcasted_iota(jnp.int32, (SLOTS, width), 0)
    c = lax.broadcasted_iota(jnp.int32, (SLOTS, width), 1)
    group = (c // LANES) ^ mine
    spread = (r == group * OWN + (c % LANES) // ROWS).astype(jnp.float32)
    for k in range(nk):
        theta = (2.0 * math.pi) * (kv_ref[nk * mine + k, 0] * g0 + kv_ref[nk * mine + k, 1] * g1)
        for dst, val in ((ce, jnp.cos(theta)), (se, jnp.sin(theta))):
            wide = lax.dot_general(
                jnp.where(live, val, 0.0), spread, (((0,), (0,)), ((), ())),
                precision=lax.Precision.HIGHEST, preferred_element_type=jnp.float32)
            for g in range(4):
                top = (g * nk + k) * atoms
                dst[top:top + atoms, :] = wide[:, g * LANES:(g + 1) * LANES]
    pad = bf.shape[0] // 4
    for g, piece in enumerate((b0, b1, b2, b3)):
        bf[g * pad:g * pad + atoms * NO, :] = piece[...].astype(jnp.float32)

    def one(a, carry):
        for g in range(4):
            lanes = slice(g * LANES, (g + 1) * LANES)
            block = bf[pl.ds(g * pad + a * NO, ROWS), :]
            for k in range(nk):
                row = pl.multiple_of((a * nk + k) * 2 * ROWS, 2 * ROWS)
                h_ref[pl.ds(row, ROWS), lanes] = (ce[pl.ds((g * nk + k) * atoms + a, 1), :] * block).astype(jnp.bfloat16)
                h_ref[pl.ds(row + ROWS, ROWS), lanes] = (se[pl.ds((g * nk + k) * atoms + a, 1), :] * block).astype(jnp.bfloat16)
        return carry

    lax.fori_loop(0, atoms, one, 0)


def phase_blocks(kvecs, spot, offsets, counts, pieces, nk):
    atoms = offsets.shape[0]
    return pl.pallas_call(
        phase_kernel,
        out_shape=jax.ShapeDtypeStruct((nk * atoms * 2 * ROWS, 4 * LANES), jnp.bfloat16),
        in_specs=[SMEM, SMEM] + [VMEM] * 6,
        out_specs=VMEM,
        scratch_shapes=[pltpu.VMEM((4 * nk * atoms, LANES), jnp.float32)] * 2
        + [pltpu.VMEM((4 * (atoms * NO + 4), LANES), jnp.float32)],
        name="phase_blocks",
    )(kvecs, spot, offsets.T, counts.reshape(1, atoms), *pieces)


def apply_kernel(nbr_ref, spot_ref, h_ref, own_ref, a_ref, b_ref, *rest, halos):
    if halos:
        out_ref, send_a, send_b, flat, win, acc = rest
    else:
        out_ref, flat, win, acc = rest
    atoms = nbr_ref.shape[1]
    nk = h_ref.shape[0] // (atoms * 2 * ROWS)
    window = atoms + 2 * REACH
    edge = REACH * 2 * NO
    mid = atoms * 2 * NO
    span = edge * 2 + mid
    mine = spot_ref[0]
    odd = spot_ref[1]
    right = edge + mid
    for k in range(nk):
        to_a = pl.multiple_of(k * span + odd * right, 8)
        to_b = pl.multiple_of(k * span + (1 - odd) * right, 8)
        flat[pl.ds(to_a, edge), :] = a_ref[k * edge:(k + 1) * edge, :].astype(jnp.float32)
        flat[pl.ds(to_b, edge), :] = b_ref[k * edge:(k + 1) * edge, :].astype(jnp.float32)
        flat[k * span + edge:k * span + edge + mid, :] = own_ref[k * mid:(k + 1) * mid, :].astype(jnp.float32)
    flat[nk * span:, :] = jnp.zeros((flat.shape[0] - nk * span, NV), jnp.float32)

    def split(i, carry):
        for j in range(SPLIT):
            w = i * SPLIT + j
            for k in range(nk):
                for part in range(2):
                    rows = flat[pl.ds(k * span + w * 2 * NO + part, ROWS, stride=2), :]
                    win[w, k, part] = rows.astype(jnp.bfloat16)
        return carry

    lax.fori_loop(0, window // SPLIT, split, 0)

    def some(i, carry):
        for j in range(UNROLL):
            a = i * UNROLL + j
            spots = [nbr_ref[(mine ^ g) * OWN + s, a] for g in range(4) for s in range(OWN)]
            for k in range(nk):
                row = pl.multiple_of((a * nk + k) * 2 * ROWS, 2 * ROWS)
                total = None
                for half in range(2):
                    tiles = [jnp.concatenate([win[w, k, 0], win[w, k, 1]], axis=1)
                             for w in spots[half * 2 * OWN:(half + 1) * 2 * OWN]]
                    rhs = jnp.concatenate(tiles, axis=0)
                    lhs = h_ref[pl.ds(row, 2 * ROWS), 2 * half * LANES:(2 * half + 2) * LANES]
                    got = jnp.dot(lhs, rhs, preferred_element_type=jnp.float32)
                    total = got if total is None else total + got
                re = total[:ROWS, :NV] - total[ROWS:, NV:]
                im = total[:ROWS, NV:] + total[ROWS:, :NV]
                start = (k * atoms + a) * 2 * NO
                acc[pl.ds(start, NO, stride=2), :] = re[:NO]
                acc[pl.ds(start + 1, NO, stride=2), :] = im[:NO]
        return carry

    lax.fori_loop(0, atoms // UNROLL, some, 0)
    out_ref[...] = acc[...].astype(jnp.bfloat16)
    if halos:
        for k in range(nk):
            top = pl.multiple_of(k * mid + odd * (mid - edge), 8)
            send_a[k * edge:(k + 1) * edge, :] = acc[pl.ds(top, edge), :].astype(jnp.bfloat16)
            top = pl.multiple_of(k * mid + (1 - odd) * (mid - edge), 8)
            send_b[k * edge:(k + 1) * edge, :] = acc[pl.ds(top, edge), :].astype(jnp.bfloat16)


def apply_blocks(nbr, spot, h, own, from_a, from_b, halos):
    atoms = nbr.shape[1]
    nk = h.shape[0] // (atoms * 2 * ROWS)
    edge = nk * REACH * 2 * NO
    window = atoms + 2 * REACH
    shapes = [jax.ShapeDtypeStruct(own.shape, jnp.bfloat16)]
    if halos:
        shapes += [jax.ShapeDtypeStruct((edge, NV), jnp.bfloat16)] * 2
    return pl.pallas_call(
        lambda *refs: apply_kernel(*refs, halos=halos),
        out_shape=shapes,
        in_specs=[SMEM, SMEM] + [VMEM] * 4,
        out_specs=[VMEM] * len(shapes),
        scratch_shapes=[
            pltpu.VMEM((nk * window * 2 * NO + ROWS, NV), jnp.float32),
            pltpu.VMEM((window, nk, 2, ROWS, NV), jnp.bfloat16),
            pltpu.VMEM((own.shape[0], NV), jnp.float32),
        ],
        name="apply_blocks",
    )(nbr, spot, h, own, from_a, from_b)


def exchange(send_a, send_b):
    n = lax.axis_size("atoms")
    across = [(i, (i + 1) % n if i % 2 else (i - 1) % n) for i in range(n)]
    return (lax.ppermute(send_a, "atoms", across),
            lax.ppermute(send_b, "atoms", [(i, i ^ 1) for i in range(n)]))


def per_device(blocks, vectors, kvecs, neighbours, offsets, counts):
    atoms = blocks.shape[0]
    nk = vectors.shape[0]
    at = lax.axis_index("atoms").astype(jnp.int32)
    odd = at % 2
    rows = jnp.transpose(vectors, (0, 1, 3, 2, 4)).reshape(nk * atoms * NO * 2, NV)
    per_k = rows.reshape(nk, atoms * NO * 2, NV)
    edge = REACH * NO * 2
    rest = atoms * NO * 2 - edge
    packed = pack_blocks(blocks)
    owners = lax.axis_size("kpt")
    pieces = [packed] + [
        lax.ppermute(packed, "kpt", [(i, i ^ d) for i in range(owners)]) for d in range(1, owners)
    ]
    from_a, from_b = exchange(
        lax.dynamic_slice_in_dim(per_k, odd * rest, edge, 1).reshape(nk * edge, NV),
        lax.dynamic_slice_in_dim(per_k, (1 - odd) * rest, edge, 1).reshape(nk * edge, NV))
    spot = jnp.stack([lax.axis_index("kpt").astype(jnp.int32), odd])
    total_atoms = atoms * lax.axis_size("atoms")
    nbr = (neighbours.T - (at * atoms - REACH) + total_atoms) % total_atoms
    h = phase_blocks(kvecs, spot, offsets, counts, pieces, nk)
    first, send_a, send_b = apply_blocks(nbr, spot, h, rows, from_a, from_b, True)
    from_a, from_b = exchange(send_a, send_b)
    (second,) = apply_blocks(nbr, spot, h, first, from_a, from_b, False)

    def whole(flat):
        return jnp.transpose(flat.reshape(nk, atoms, NO, 2, NV), (0, 1, 3, 2, 4))

    return whole(first), whole(second)


def solution(mesh):
    placed = (
        P("atoms", "kpt", None, None),
        P("kpt", "atoms", None, None, None),
        P(),
        P("atoms", None),
        P("atoms", None),
        P("atoms"),
    )
    return jax.shard_map(
        per_device,
        mesh=mesh,
        in_specs=placed,
        out_specs=(P("kpt", "atoms", None, None, None), P("kpt", "atoms", None, None, None)),
        check_vma=False,
    )
```

```python
import math

import jax
import jax.numpy as jnp
from jax import lax
from jax.experimental import pallas as pl
from jax.experimental.pallas import tpu as pltpu
from jax.sharding import PartitionSpec as P


REACH = 32
NO = 13
NV = 128
OWN = 8
LANES = 128
ROWS = 16
SPLIT = 4
UNROLL = 4
VMEM = pl.BlockSpec(memory_space=pltpu.VMEM)
SMEM = pl.BlockSpec(memory_space=pltpu.SMEM)
PARAMS = pltpu.CompilerParams(vmem_limit_bytes=24 << 20)


def near(array):
    return pltpu.with_memory_space_constraint(array, pltpu.VMEM)


def pack_kernel(blocks_ref, out_ref, buf):
    atoms = blocks_ref.shape[3]
    r = lax.broadcasted_iota(jnp.int32, (NO * OWN, LANES), 0)
    c = lax.broadcasted_iota(jnp.int32, (NO * OWN, LANES), 1)
    place = ((r % OWN == c // ROWS) & (r // OWN == c % ROWS)).astype(jnp.float32).astype(jnp.bfloat16)
    for x in range(NO):
        b = blocks_ref[x].astype(jnp.float32).reshape(NO * OWN, atoms).astype(jnp.bfloat16)
        t = lax.dot_general(b, place, (((0,), (0,)), ((), ())), preferred_element_type=jnp.float32)
        buf[pl.ds(x, atoms, stride=NO), :] = t
    out_ref[...] = buf[...].astype(jnp.bfloat16)


def pack_blocks(blocks):
    atoms = blocks.shape[0]
    return pl.pallas_call(
        pack_kernel,
        out_shape=pltpu.VMEM((atoms * NO, LANES), jnp.bfloat16),
        in_specs=[VMEM],
        out_specs=VMEM,
        scratch_shapes=[pltpu.VMEM((atoms * NO, LANES), jnp.float32)],
        name="pack_blocks",
        compiler_params=PARAMS,
    )(jnp.transpose(blocks, (2, 3, 1, 0)))


def trig_kernel(kv_ref, nbr_ref, offs_ref, counts_ref, ce, se, local_ref):
    slots, atoms = offs_ref.shape
    nk = ce.shape[0] // (4 * atoms)
    mine = lax.axis_index("kpt")
    at = lax.axis_index("atoms")
    total = atoms * lax.axis_size("atoms")
    place = nbr_ref[...] - (at * atoms - REACH)
    place = jnp.where(place < 0, place + total, place)
    local_ref[...] = jnp.where(place >= total, place - total, place)
    offs = offs_ref[...]
    g0 = (offs // 7 - 3).astype(jnp.float32)
    g1 = (offs % 7 - 3).astype(jnp.float32)
    slot = lax.broadcasted_iota(jnp.int32, offs.shape, 0)
    live = slot < counts_ref[...]
    width = 4 * LANES
    r = lax.broadcasted_iota(jnp.int32, (slots, width), 0)
    c = lax.broadcasted_iota(jnp.int32, (slots, width), 1)
    group = (c // LANES) ^ mine
    spread = (r == group * OWN + (c % LANES) // ROWS).astype(jnp.float32)
    for k in range(nk):
        theta = (2.0 * math.pi) * (kv_ref[0, nk * mine + k] * g0 + kv_ref[1, nk * mine + k] * g1)
        for dst, val in ((ce, jnp.cos(theta)), (se, jnp.sin(theta))):
            wide = lax.dot_general(
                jnp.where(live, val, 0.0), spread, (((0,), (0,)), ((), ())),
                precision=lax.Precision.HIGHEST, preferred_element_type=jnp.float32)
            for g in range(4):
                top = (g * nk + k) * atoms
                dst[top:top + atoms, :] = wide[:, g * LANES:(g + 1) * LANES]


def trig(kvecs, neighbours, offsets, counts, nk):
    atoms, slots = offsets.shape
    wide = pltpu.VMEM((4 * nk * atoms, LANES), jnp.float32)
    return pl.pallas_call(
        trig_kernel,
        out_shape=[wide, wide, jax.ShapeDtypeStruct((slots, atoms), jnp.int32)],
        in_specs=[SMEM] + [VMEM] * 3,
        out_specs=[VMEM] * 3,
        name="trig",
        compiler_params=PARAMS,
    )(kvecs.T, neighbours.T, offsets.T, counts.reshape(1, atoms))


def phase_kernel(ce, se, b0, b1, b2, b3, h_ref, bf):
    atoms = b0.shape[0] // NO
    nk = h_ref.shape[0] // (atoms * 2 * ROWS)
    pad = bf.shape[0] // 4
    for g, piece in enumerate((b0, b1, b2, b3)):
        bf[g * pad:g * pad + atoms * NO, :] = piece[...].astype(jnp.float32)

    def some(i, carry):
        for j in range(2):
            a = i * 2 + j
            for g in range(4):
                lanes = slice(g * LANES, (g + 1) * LANES)
                block = bf[pl.ds(g * pad + a * NO, ROWS), :]
                for k in range(nk):
                    row = pl.multiple_of((a * nk + k) * 2 * ROWS, 2 * ROWS)
                    top = (g * nk + k) * atoms + a
                    h_ref[pl.ds(row, ROWS), lanes] = (ce[pl.ds(top, 1), :] * block).astype(jnp.bfloat16)
                    h_ref[pl.ds(row + ROWS, ROWS), lanes] = (se[pl.ds(top, 1), :] * block).astype(jnp.bfloat16)
        return carry

    lax.fori_loop(0, atoms // 2, some, 0)


def phase_blocks(ce, se, pieces, atoms, nk):
    return pl.pallas_call(
        phase_kernel,
        out_shape=pltpu.VMEM((nk * atoms * 2 * ROWS, 4 * LANES), jnp.bfloat16),
        in_specs=[VMEM] * 6,
        out_specs=VMEM,
        scratch_shapes=[pltpu.VMEM((4 * (atoms * NO + 4), LANES), jnp.float32)],
        name="phase_blocks",
        compiler_params=PARAMS,
    )(near(ce), near(se), *[near(p) for p in pieces])


def apply_kernel(nbr_ref, h_ref, own_ref, a_ref, b_ref, *rest, halos):
    if halos:
        out_ref, send_a, send_b, flat, win, acc = rest
    else:
        out_ref, flat, win, acc = rest
    atoms = nbr_ref.shape[1]
    nk = h_ref.shape[0] // (atoms * 2 * ROWS)
    window = atoms + 2 * REACH
    edge = REACH * 2 * NO
    mid = atoms * 2 * NO
    span = edge * 2 + mid
    mine = lax.axis_index("kpt")
    odd = lax.axis_index("atoms") % 2
    right = edge + mid
    for k in range(nk):
        to_a = pl.multiple_of(k * span + odd * right, 8)
        to_b = pl.multiple_of(k * span + (1 - odd) * right, 8)
        flat[pl.ds(to_a, edge), :] = a_ref[k * edge:(k + 1) * edge, :].astype(jnp.float32)
        flat[pl.ds(to_b, edge), :] = b_ref[k * edge:(k + 1) * edge, :].astype(jnp.float32)
        flat[k * span + edge:k * span + edge + mid, :] = own_ref[k * mid:(k + 1) * mid, :].astype(jnp.float32)
    flat[nk * span:, :] = jnp.zeros((flat.shape[0] - nk * span, NV), jnp.float32)

    def split(i, carry):
        for j in range(SPLIT):
            w = i * SPLIT + j
            for k in range(nk):
                for part in range(2):
                    rows = flat[pl.ds(k * span + w * 2 * NO + part, ROWS, stride=2), :]
                    win[w, k, part] = rows.astype(jnp.bfloat16)
        return carry

    lax.fori_loop(0, window // SPLIT, split, 0)

    def some(i, carry):
        for j in range(UNROLL):
            a = i * UNROLL + j
            spots = [nbr_ref[(mine ^ g) * OWN + s, a] for g in range(4) for s in range(OWN)]
            for k in range(nk):
                row = pl.multiple_of((a * nk + k) * 2 * ROWS, 2 * ROWS)
                total = None
                for half in range(2):
                    tiles = [jnp.concatenate([win[w, k, 0], win[w, k, 1]], axis=1)
                             for w in spots[half * 2 * OWN:(half + 1) * 2 * OWN]]
                    rhs = jnp.concatenate(tiles, axis=0)
                    lhs = h_ref[pl.ds(row, 2 * ROWS), 2 * half * LANES:(2 * half + 2) * LANES]
                    got = jnp.dot(lhs, rhs, preferred_element_type=jnp.float32)
                    total = got if total is None else total + got
                re = total[:ROWS, :NV] - total[ROWS:, NV:]
                im = total[:ROWS, NV:] + total[ROWS:, :NV]
                start = (k * atoms + a) * 2 * NO
                acc[pl.ds(start, NO, stride=2), :] = re[:NO]
                acc[pl.ds(start + 1, NO, stride=2), :] = im[:NO]
        return carry

    lax.fori_loop(0, atoms // UNROLL, some, 0)
    out_ref[...] = acc[...].astype(jnp.bfloat16)
    if halos:
        for k in range(nk):
            top = pl.multiple_of(k * mid + odd * (mid - edge), 8)
            send_a[k * edge:(k + 1) * edge, :] = acc[pl.ds(top, edge), :].astype(jnp.bfloat16)
            top = pl.multiple_of(k * mid + (1 - odd) * (mid - edge), 8)
            send_b[k * edge:(k + 1) * edge, :] = acc[pl.ds(top, edge), :].astype(jnp.bfloat16)


def apply_blocks(nbr, h, own, from_a, from_b, halos):
    atoms = nbr.shape[1]
    nk = h.shape[0] // (atoms * 2 * ROWS)
    edge = nk * REACH * 2 * NO
    window = atoms + 2 * REACH
    shapes = [jax.ShapeDtypeStruct(own.shape, jnp.bfloat16)]
    if halos:
        shapes = [pltpu.VMEM(own.shape, jnp.bfloat16)] + [pltpu.VMEM((edge, NV), jnp.bfloat16)] * 2
    return pl.pallas_call(
        lambda *refs: apply_kernel(*refs, halos=halos),
        out_shape=shapes,
        in_specs=[SMEM] + [VMEM] * 4,
        out_specs=[VMEM] * len(shapes),
        scratch_shapes=[
            pltpu.VMEM((nk * window * 2 * NO + ROWS, NV), jnp.float32),
            pltpu.VMEM((window, nk, 2, ROWS, NV), jnp.bfloat16),
            pltpu.VMEM((own.shape[0], NV), jnp.float32),
        ],
        name="apply_blocks",
        compiler_params=PARAMS,
    )(nbr, near(h), own, near(from_a), near(from_b))


def exchange(send_a, send_b):
    n = lax.axis_size("atoms")
    across = [(i, (i + 1) % n if i % 2 else (i - 1) % n) for i in range(n)]
    from_a = lax.ppermute(send_a, "atoms", across)
    from_b = lax.ppermute(send_b, "atoms", [(i, i ^ 1) for i in range(n)])
    return from_a, from_b


def whole_step(blocks, vectors, kvecs, neighbours, offsets, counts):
    atoms = blocks.shape[0]
    nk = vectors.shape[0]
    at = lax.axis_index("atoms").astype(jnp.int32)
    odd = at % 2
    rows = jnp.transpose(vectors, (0, 1, 3, 2, 4)).reshape(nk * atoms * NO * 2, NV)
    per_k = rows.reshape(nk, atoms * NO * 2, NV)
    edge = REACH * NO * 2
    rest = atoms * NO * 2 - edge
    packed = pack_blocks(blocks)
    per_k, packed = lax.optimization_barrier((per_k, packed))
    owners = lax.axis_size("kpt")
    pieces = [packed] + [
        lax.ppermute(packed, "kpt", [(i, i ^ d) for i in range(owners)]) for d in range(1, owners)
    ]
    from_a, from_b = exchange(
        lax.dynamic_slice_in_dim(per_k, odd * rest, edge, 1).reshape(nk * edge, NV),
        lax.dynamic_slice_in_dim(per_k, (1 - odd) * rest, edge, 1).reshape(nk * edge, NV))
    ce, se, nbr = trig(kvecs, neighbours, offsets, counts, nk)
    h = phase_blocks(ce, se, pieces, atoms, nk)
    first, send_a, send_b = apply_blocks(nbr, h, rows, from_a, from_b, True)
    from_a, from_b = exchange(send_a, send_b)
    (second,) = apply_blocks(nbr, h, first, from_a, from_b, False)

    def whole(flat):
        return jnp.transpose(flat.reshape(nk, atoms, NO, 2, NV), (0, 1, 3, 2, 4))

    return whole(first), whole(second)


def solution(mesh):
    placed = (
        P("atoms", "kpt", None, None),
        P("kpt", "atoms", None, None, None),
        P(),
        P("atoms", None),
        P("atoms", None),
        P("atoms"),
    )
    return jax.shard_map(
        whole_step,
        mesh=mesh,
        in_specs=placed,
        out_specs=(P("kpt", "atoms", None, None, None), P("kpt", "atoms", None, None, None)),
        check_vma=False,
    )
```
